256 devices in a mesh: seq: 8 (over z), bal: 4 (over x), rep: 8 (over y, core).
Axes of the slice: x: 4, y: 4, z: 8, core: 2. Of those that a mesh axis runs over, the one named last changes fastest.
Arguments:
- queries: bfloat16 [32, 6, 512, 2048], P('rep', None, ('seq', 'bal')), parts along dimension 0, may hold values from -16 to 16
- key_tokens: bfloat16 [32, 6, 512, 2048], P('rep', None, ('seq', 'bal')), parts along dimension 0, may hold values from -8 to 8
- value_tokens: bfloat16 [32, 6, 512, 2048], P('rep', None, ('seq', 'bal')), parts along dimension 0, may hold values from -6 to 6
- view_lists: int32 [32, 6, 4], P('rep'), parts along dimension 0, may hold values from -1 to 5, as said below
Outputs:
- attended: bfloat16 [32, 6, 512, 2048], P('rep', None, ('seq', 'bal')), parts along dimension 0
The draws below stay inside these ranges and needn't reach their ends.
There are 8 independent parts, one for each index of `rep`. The reference program is written for one: setup_inputs(seed, part) draws one part's arguments, and reference() takes and returns one part's arrays. A program takes and returns all parts, laid end to end along the dimension named above; each array names one. Nothing has to cross between parts.
Inputs may be any that keep to these rules, and one draw needn't show every extreme that they name: Each list view_lists[w, v] begins with v itself, names distinct views, and holds -1 in every entry after its named views; in every draw some list names 4 views.
All inputs are finite; a program needn't handle non-finite values.
Results may differ from the reference program's by a relative error of at most 0.003.
Values may be sent and summed in bfloat16 or wider, within the bound.
A program may use at most 64 MiB of HBM per device.

```python
import math
import jax
import jax.numpy as jnp
from jax import lax

HEAD = 128
D = 2048
VIEWS = 6
KMAX = 4
WTOK = 512
WINDOWS = 4


def draw_queries(key, part):
    shape = (WINDOWS, VIEWS, WTOK, D)
    scale_shape = (WINDOWS, VIEWS, WTOK, 1)
    base_noise = jnp.clip(jax.random.normal(jax.random.fold_in(key, 11), shape, jnp.float32), -4.0, 4.0)
    row_scale = jnp.exp(jax.random.uniform(jax.random.fold_in(key, 12), scale_shape, jnp.float32, math.log(0.4), math.log(4.0)))
    values = base_noise * row_scale
    return values.astype(jnp.bfloat16)


def draw_key_tokens(key, part):
    shape = (WINDOWS, VIEWS, WTOK, D)
    scale_shape = (WINDOWS, VIEWS, WTOK, 1)
    base_noise = jnp.clip(jax.random.normal(jax.random.fold_in(key, 21), shape, jnp.float32), -4.0, 4.0)
    row_scale = jnp.exp(jax.random.uniform(jax.random.fold_in(key, 22), scale_shape, jnp.float32, math.log(0.5), math.log(2.0)))
    values = base_noise * row_scale
    return values.astype(jnp.bfloat16)


def one_order(sub_key):
    return jax.random.permutation(sub_key, VIEWS)


def draw_view_lists(key, part):
    dense_window = jax.random.randint(jax.random.fold_in(key, 5), (), 0, WINDOWS)
    grid_keys = jax.random.split(jax.random.fold_in(key, 6), WINDOWS * VIEWS)
    orders = jax.vmap(one_order)(grid_keys).reshape(WINDOWS, VIEWS, VIEWS).astype(jnp.int32)
    self_ids = jnp.arange(VIEWS, dtype=jnp.int32)[None, :, None]
    position = jnp.arange(VIEWS, dtype=jnp.int32)[None, None, :]
    ranking = jnp.where(orders == self_ids, -1, position)
    placement = jnp.argsort(ranking, axis=-1, stable=True)
    listed = jnp.take_along_axis(orders, placement, axis=-1)[:, :, :KMAX]
    extra = (jax.random.randint(jax.random.fold_in(key, 7), (WINDOWS, VIEWS), 0, 4) == 0).astype(jnp.int32)
    window_ids = jnp.arange(WINDOWS, dtype=jnp.int32)[:, None]
    lengths = jnp.where(window_ids == dense_window, KMAX, 1 + extra)
    slot_ids = jnp.arange(KMAX, dtype=jnp.int32)[None, None, :]
    return jnp.where(slot_ids < lengths[:, :, None], listed, -1).astype(jnp.int32)


def block_scale(stream_key, shape, cuts, smallest, high):
    def one(dim, parts):
        draws = jax.random.uniform(jax.random.fold_in(jax.random.fold_in(stream_key, 6), dim), (parts,), jnp.float32, smallest / len(cuts), high / len(cuts))
        return jnp.repeat(jnp.exp(draws), shape[dim] // parts).reshape((-1,) + (1,) * (len(shape) - dim - 1))

    level = one(*cuts[0])
    for cut in cuts[1:]:
        level = level * one(*cut)
    return level


def bell_draw(rng, dims, spread, reach, shards=(), kind=jnp.bfloat16):
    values = spread * jax.random.normal(rng, dims, jnp.float32)
    if shards:
        values = values * block_scale(rng, dims, shards, -0.22, 0.18)
    return jnp.clip(values, -reach, reach).astype(kind)


def setup_inputs(seed: int = 0, part: int = 0) -> dict:
    key_of = jax.random.split(jax.random.key(seed), 5)
    part_splits = jax.random.split(jax.random.fold_in(key_of[4], part), 5)
    return {
        "queries": draw_queries(jax.random.fold_in(jax.random.fold_in(key_of[4], part), 71), part),
        "key_tokens": draw_key_tokens(jax.random.fold_in(jax.random.fold_in(key_of[4], part), 71), part),
        "value_tokens": bell_draw(part_splits[2], (WINDOWS, VIEWS, WTOK, D), 1.0, 6.0, ((2, 32),)),
        "view_lists": draw_view_lists(jax.random.fold_in(jax.random.fold_in(key_of[4], part), 71), part),
    }


def reference(queries, key_tokens, value_tokens, view_lists):
    windows, view_count, row_count, feature_width = queries.shape
    head_count = feature_width // HEAD
    score_scale = 1.0 / math.sqrt(HEAD)
    view_ids = jnp.arange(view_count, dtype=jnp.int32)
    outputs = []
    for window in range(windows):
        key_all = key_tokens[window].astype(jnp.float32).reshape(view_count * row_count, head_count, HEAD)
        value_all = value_tokens[window].astype(jnp.float32).reshape(view_count * row_count, head_count, HEAD)
        per_view = []
        for view in range(view_count):
            view_row = view_lists[window, view]
            allowed = jnp.any(view_row[:, None] == view_ids[None, :], axis=0)
            key_mask = jnp.repeat(allowed, row_count)
            query_rows = queries[window, view].astype(jnp.float32).reshape(row_count, head_count, HEAD)
            scores = jnp.einsum('qhd,khd->hqk', query_rows, key_all) * score_scale
            scores = jnp.where(key_mask[None, None, :], scores, -jnp.inf)
            row_top = lax.optimization_barrier(jnp.max(scores, axis=2))
            exponent = jnp.exp(scores - row_top[:, :, None])
            row_total = lax.optimization_barrier(jnp.sum(exponent, axis=2))
            weights = lax.optimization_barrier(exponent.astype(jnp.bfloat16))
            mixed = jnp.einsum('hqk,khd->qhd', weights.astype(jnp.float32), value_all)
            mixed = mixed / jnp.transpose(row_total)[:, :, None]
            per_view.append(mixed.reshape(row_count, feature_width).astype(jnp.bfloat16))
        outputs.append(jnp.stack(per_view))
    return jnp.stack(outputs)
```

```python
import functools
import math

import jax
import jax.numpy as jnp
from jax import lax
from jax.experimental import pallas as pl
from jax.experimental.pallas import tpu as pltpu
from jax.sharding import PartitionSpec as P

HEAD = 128
QUERY_BLOCK = 256
MESH = pl.DeviceIdType.MESH
ROWS_BY_ROWS = (((1,), (1,)), ((), ()))
EXP2_SCALE = math.log2(math.e) / math.sqrt(HEAD)


def attend(view_lists, window, view, query_buf, key_buf, value_buf, result_buf):
    slots = view_lists.shape[2]
    rows = query_buf.shape[1]
    entries = [view_lists[window, view, slot] for slot in range(slots)]
    named = [jnp.where(entry >= 0, 1.0, 0.0).astype(jnp.float32) for entry in entries]
    key_views = [jnp.where(entry >= 0, entry, view) for entry in entries]

    def block(index, carry):
        span = pl.ds(pl.multiple_of(index * QUERY_BLOCK, QUERY_BLOCK), QUERY_BLOCK)
        query_rows = query_buf[view, span, :]
        scores = [
            lax.dot_general(query_rows, key_buf[u], ROWS_BY_ROWS, preferred_element_type=jnp.float32)
            for u in key_views
        ]
        top = functools.reduce(jnp.maximum, scores)
        top = jnp.max(top, axis=1, keepdims=True) * EXP2_SCALE
        total = jnp.zeros((QUERY_BLOCK, 1), jnp.float32)
        mixed = jnp.zeros((QUERY_BLOCK, HEAD), jnp.float32)
        for slot, u in enumerate(key_views):
            exponent = jnp.exp2(scores[slot] * EXP2_SCALE - top)
            total += jnp.sum(exponent, axis=1, keepdims=True) * named[slot]
            values = value_buf[u] * named[slot].astype(jnp.bfloat16)
            mixed += jnp.dot(exponent.astype(jnp.bfloat16), values, preferred_element_type=jnp.float32)
        result_buf[view, span, :] = (mixed / total).astype(jnp.bfloat16)
        return carry

    lax.fori_loop(0, rows // QUERY_BLOCK, block, 0)


def kernel(
    seq_count, bal_count,
    view_lists, queries, keys, values,
    out,
    q0, q1, k0, k1, v0, v1, r0, r1,
    send_in, recv_in, send_out, recv_out,
):
    seq, bal = lax.axis_index("seq"), lax.axis_index("bal")
    peers = seq_count * bal_count
    me = seq * bal_count + bal
    shard = queries.shape[2]
    views = queries.shape[1]
    heads = 2
    window_rows = peers * shard

    def place(peer):
        return lax.div(peer, bal_count), lax.rem(peer, bal_count)

    def device(peer):
        peer_seq, peer_bal = place(peer)
        return {"seq": peer_seq, "bal": peer_bal}

    def rows_of(peer):
        return pl.ds(pl.multiple_of(peer * shard, shard), shard)

    def columns_of(peer_seq, head):
        return pl.ds(pl.multiple_of(peer_seq * (heads * HEAD) + head * HEAD, HEAD), HEAD)

    barrier = pltpu.get_barrier_semaphore()

    def greet(offset, carry):
        pl.semaphore_signal(
            barrier, inc=1, device_id=device(lax.rem(me + offset, peers)), device_id_type=MESH
        )
        return carry

    lax.fori_loop(1, peers, greet, 0)
    pl.semaphore_wait(barrier, peers - 1)

    inbound = []
    for head, group in enumerate(((k0, v0, q0), (k1, v1, q1))):
        for kind, (source, landing) in enumerate(zip((keys, values, queries), group)):
            inbound.append((head, 3 * head + kind, source, landing))

    for head, number, source, landing in inbound:

        def send(offset, carry):
            peer = lax.rem(me + offset, peers)
            peer_seq, peer_bal = place(peer)
            pltpu.make_async_remote_copy(
                src_ref=source.at[peer_bal, :, :, columns_of(peer_seq, head)],
                dst_ref=landing.at[:, rows_of(me), :],
                send_sem=send_in.at[number],
                recv_sem=recv_in.at[number],
                device_id=device(peer),
                device_id_type=MESH,
            ).start()
            return carry

        lax.fori_loop(1, peers, send, 0)
        pltpu.make_async_copy(
            source.at[bal, :, :, columns_of(seq, head)], landing.at[:, rows_of(me), :], recv_in.at[number]
        ).start()

    for head, landings, result in ((0, (k0, v0, q0), r0), (1, (k1, v1, q1), r1)):
        for kind, landing in enumerate(landings):
            pltpu.make_async_copy(landing, landing, recv_in.at[3 * head + kind]).wait()

        def one_view(view, carry):
            attend(view_lists, bal, view, landings[2], landings[0], landings[1], result)

            def give_back(offset, inner):
                peer = lax.rem(me + offset, peers)
                pltpu.make_async_remote_copy(
                    src_ref=result.at[view, rows_of(peer), :],
                    dst_ref=out.at[bal, view, :, columns_of(seq, head)],
                    send_sem=send_out,
                    recv_sem=recv_out,
                    device_id=device(peer),
                    device_id_type=MESH,
                ).start()
                return inner

            lax.fori_loop(1, peers, give_back, 0)
            pltpu.make_async_copy(
                result.at[view, rows_of(me), :], out.at[bal, view, :, columns_of(seq, head)], recv_out
            ).start()
            return carry

        lax.fori_loop(0, views, one_view, 0)

    pltpu.make_async_copy(out, out, recv_out).wait()
    for head, number, source, landing in inbound:
        sent = landing.at[:, pl.ds(0, window_rows - shard), :]
        pltpu.make_async_copy(sent, sent, send_in.at[number]).wait()
    for result in (r0, r1):
        sent = result.at[:, pl.ds(0, window_rows - shard), :]
        pltpu.make_async_copy(sent, sent, send_out).wait()


def local(seq_count, bal_count, queries, key_tokens, value_tokens, view_lists):
    windows, views, shard, width = queries.shape
    window_rows = seq_count * bal_count * shard
    head_buffer = pltpu.VMEM((views, window_rows, HEAD), jnp.bfloat16)
    return pl.pallas_call(
        functools.partial(kernel, seq_count, bal_count),
        out_shape=jax.ShapeDtypeStruct(queries.shape, jnp.bfloat16),
        in_specs=[pl.BlockSpec(memory_space=pltpu.SMEM)] + [pl.BlockSpec(memory_space=pl.ANY)] * 3,
        out_specs=pl.BlockSpec(memory_space=pl.ANY),
        scratch_shapes=[head_buffer] * 8
        + [
            pltpu.SemaphoreType.DMA((6,)),
            pltpu.SemaphoreType.DMA((6,)),
            pltpu.SemaphoreType.DMA,
            pltpu.SemaphoreType.DMA,
        ],
        compiler_params=pltpu.CompilerParams(
            collective_id=0, has_side_effects=True, vmem_limit_bytes=48 * 2**20
        ),
    )(view_lists, queries, key_tokens, value_tokens)


def solution(mesh):
    spec = P("rep", None, ("seq", "bal"), None)
    return jax.shard_map(
        functools.partial(local, mesh.shape["seq"], mesh.shape["bal"]),
        mesh=mesh,
        in_specs=(spec, spec, spec, P("rep", None, None)),
        out_specs=spec,
        check_vma=False,
    )
```

```python
import functools
import math

import jax
import jax.numpy as jnp
from jax import lax
from jax.experimental import pallas as pl
from jax.experimental.pallas import tpu as pltpu
from jax.sharding import PartitionSpec as P

HEAD = 128
QUERY_BLOCK = 256
MESH = pl.DeviceIdType.MESH
ROWS_BY_ROWS = (((1,), (1,)), ((), ()))
EXP2_SCALE = math.log2(math.e) / math.sqrt(HEAD)


def attend(view_lists, window, view, query_buf, key_buf, value_buf, result_buf):
    slots = view_lists.shape[1]
    rows = query_buf.shape[1]
    entries = [view_lists[window, slot, view] for slot in range(slots)]
    named = [jnp.where(entry >= 0, 1.0, 0.0).astype(jnp.float32) for entry in entries]
    key_views = [jnp.where(entry >= 0, entry, view) for entry in entries]

    def block(index, carry):
        span = pl.ds(pl.multiple_of(index * QUERY_BLOCK, QUERY_BLOCK), QUERY_BLOCK)
        query_rows = query_buf[view, span, :]
        scores = [
            lax.dot_general(query_rows, key_buf[u], ROWS_BY_ROWS, preferred_element_type=jnp.float32)
            for u in key_views
        ]
        top = functools.reduce(jnp.maximum, scores)
        top = jnp.max(top, axis=1, keepdims=True) * EXP2_SCALE
        total = jnp.zeros((QUERY_BLOCK, 1), jnp.float32)
        mixed = jnp.zeros((QUERY_BLOCK, HEAD), jnp.float32)
        for slot, u in enumerate(key_views):
            exponent = jnp.exp2(scores[slot] * EXP2_SCALE - top)
            total += jnp.sum(exponent, axis=1, keepdims=True) * named[slot]
            values = value_buf[u] * named[slot].astype(jnp.bfloat16)
            mixed += jnp.dot(exponent.astype(jnp.bfloat16), values, preferred_element_type=jnp.float32)
        result_buf[view, span, :] = (mixed / total).astype(jnp.bfloat16)
        return carry

    lax.fori_loop(0, rows // QUERY_BLOCK, block, 0)


def kernel(
    seq_count, bal_count,
    view_lists, queries, keys, values,
    out,
    q0, q1, k0, k1, v0, v1, r0, r1,
    send_in, recv_in, send_out, recv_out,
):
    seq, bal = lax.axis_index("seq"), lax.axis_index("bal")
    peers = seq_count * bal_count
    me = seq * bal_count + bal
    shard = queries.shape[2]
    views = queries.shape[1]
    heads = 2
    window_rows = peers * shard

    def place(peer):
        return lax.div(peer, bal_count), lax.rem(peer, bal_count)

    def device(peer):
        peer_seq, peer_bal = place(peer)
        return {"seq": peer_seq, "bal": peer_bal}

    def rows_of(peer):
        return pl.ds(pl.multiple_of(peer * shard, shard), shard)

    def columns_of(peer_seq, head):
        return pl.ds(pl.multiple_of(peer_seq * (heads * HEAD) + head * HEAD, HEAD), HEAD)

    barrier = pltpu.get_barrier_semaphore()

    def greet(offset, carry):
        pl.semaphore_signal(
            barrier, inc=1, device_id=device(lax.rem(me + offset, peers)), device_id_type=MESH
        )
        return carry

    lax.fori_loop(1, peers, greet, 0)
    pl.semaphore_wait(barrier, peers - 1)

    inbound = []
    for head, group in enumerate(((k0, v0, q0), (k1, v1, q1))):
        for kind, (source, landing) in enumerate(zip((keys, values, queries), group)):
            inbound.append((head, 3 * head + kind, source, landing))

    for head, number, source, landing in inbound:

        def send(offset, carry):
            peer = lax.rem(me + offset, peers)
            peer_seq, peer_bal = place(peer)
            pltpu.make_async_remote_copy(
                src_ref=source.at[peer_bal, :, :, columns_of(peer_seq, head)],
                dst_ref=landing.at[:, rows_of(me), :],
                send_sem=send_in.at[number],
                recv_sem=recv_in.at[number],
                device_id=device(peer),
                device_id_type=MESH,
            ).start()
            return carry

        lax.fori_loop(1, peers, send, 0)
        pltpu.make_async_copy(
            source.at[bal, :, :, columns_of(seq, head)], landing.at[:, rows_of(me), :], recv_in.at[number]
        ).start()

    for head, landings, result in ((0, (k0, v0, q0), r0), (1, (k1, v1, q1), r1)):
        for kind, landing in enumerate(landings):
            pltpu.make_async_copy(landing, landing, recv_in.at[3 * head + kind]).wait()

        def one_view(view, carry):
            attend(view_lists, bal, view, landings[2], landings[0], landings[1], result)

            def give_back(offset, inner):
                peer = lax.rem(me + offset, peers)
                pltpu.make_async_remote_copy(
                    src_ref=result.at[view, rows_of(peer), :],
                    dst_ref=out.at[bal, view, :, columns_of(seq, head)],
                    send_sem=send_out,
                    recv_sem=recv_out,
                    device_id=device(peer),
                    device_id_type=MESH,
                ).start()
                return inner

            lax.fori_loop(1, peers, give_back, 0)
            pltpu.make_async_copy(
                result.at[view, rows_of(me), :], out.at[bal, view, :, columns_of(seq, head)], recv_out
            ).start()
            return carry

        lax.fori_loop(0, views, one_view, 0)

    pltpu.make_async_copy(out, out, recv_out).wait()
    for head, number, source, landing in inbound:
        sent = landing.at[:, pl.ds(0, window_rows - shard), :]
        pltpu.make_async_copy(sent, sent, send_in.at[number]).wait()
    for result in (r0, r1):
        sent = result.at[:, pl.ds(0, window_rows - shard), :]
        pltpu.make_async_copy(sent, sent, send_out).wait()


def local(seq_count, bal_count, queries, key_tokens, value_tokens, view_lists):
    windows, views, shard, width = queries.shape
    window_rows = seq_count * bal_count * shard
    head_buffer = pltpu.VMEM((views, window_rows, HEAD), jnp.bfloat16)
    return pl.pallas_call(
        functools.partial(kernel, seq_count, bal_count),
        out_shape=pltpu.VMEM(queries.shape, jnp.bfloat16),
        in_specs=[pl.BlockSpec(memory_space=pltpu.SMEM)] + [pl.BlockSpec(memory_space=pl.ANY)] * 3,
        scratch_shapes=[head_buffer] * 8
        + [
            pltpu.SemaphoreType.DMA((6,)),
            pltpu.SemaphoreType.DMA((6,)),
            pltpu.SemaphoreType.DMA,
            pltpu.SemaphoreType.DMA,
        ],
        compiler_params=pltpu.CompilerParams(
            collective_id=0, has_side_effects=True, vmem_limit_bytes=62 * 2**20
        ),
    )(jnp.swapaxes(view_lists, 1, 2), queries, key_tokens, value_tokens)


def solution(mesh):
    spec = P("rep", None, ("seq", "bal"), None)
    return jax.shard_map(
        functools.partial(local, mesh.shape["seq"], mesh.shape["bal"]),
        mesh=mesh,
        in_specs=(spec, spec, spec, P("rep", None, None)),
        out_specs=spec,
        check_vma=False,
    )
```

```python
import functools
import math

import jax
import jax.numpy as jnp
from jax import lax
from jax.experimental import pallas as pl
from jax.experimental.pallas import tpu as pltpu
from jax.sharding import PartitionSpec as P

HEAD = 128
QUERY_BLOCK = 256
MESH = pl.DeviceIdType.MESH
ROWS_BY_ROWS = (((1,), (1,)), ((), ()))
EXP2_SCALE = math.log2(math.e) / math.sqrt(HEAD)


def attend(view_lists, window, view, query_buf, key_buf, value_buf, result_buf):
    slots = view_lists.shape[1]
    rows = query_buf.shape[1]
    entries = [view_lists[window, slot, view] for slot in range(slots)]
    named = [jnp.where(entry >= 0, 1.0, 0.0).astype(jnp.float32) for entry in entries]
    key_views = [jnp.where(entry >= 0, entry, view) for entry in entries]

    def block(index, carry):
        span = pl.ds(pl.multiple_of(index * QUERY_BLOCK, QUERY_BLOCK), QUERY_BLOCK)
        query_rows = query_buf[view, span, :]
        scores = [
            lax.dot_general(query_rows, key_buf[u], ROWS_BY_ROWS, preferred_element_type=jnp.float32)
            for u in key_views
        ]
        top = functools.reduce(jnp.maximum, scores)
        top = jnp.max(top, axis=1, keepdims=True) * EXP2_SCALE
        total = jnp.zeros((QUERY_BLOCK, 1), jnp.float32)
        mixed = jnp.zeros((QUERY_BLOCK, HEAD), jnp.float32)
        for slot, u in enumerate(key_views):
            exponent = jnp.exp2(scores[slot] * EXP2_SCALE - top)
            total += jnp.sum(exponent, axis=1, keepdims=True) * named[slot]
            values = value_buf[u] * named[slot].astype(jnp.bfloat16)
            mixed += jnp.dot(exponent.astype(jnp.bfloat16), values, preferred_element_type=jnp.float32)
        result_buf[view, span, :] = (mixed / total).astype(jnp.bfloat16)
        return carry

    lax.fori_loop(0, rows // QUERY_BLOCK, block, 0)


def kernel(
    seq_count, bal_count,
    lists_in, queries, keys, values,
    out,
    q0, q1, k0, k1, v0, v1, r0, r1,
    send_in, recv_in, send_out, recv_out, columns_in,
    view_lists, lists_sem,
):
    seq, bal = lax.axis_index("seq"), lax.axis_index("bal")
    peers = seq_count * bal_count
    me = seq * bal_count + bal
    shard = queries.shape[2]
    views = queries.shape[1]
    heads = 2
    window_rows = peers * shard

    def loop(first, last, body):
        def run(index, carry):
            body(index)
            return carry

        lax.fori_loop(first, last, run, 0)

    def at(along_seq, along_bal):
        return lax.rem(seq + along_seq, seq_count), lax.rem(bal + along_bal, bal_count)

    def device(peer):
        return {"seq": peer[0], "bal": peer[1]}

    def rows_of(number):
        return pl.ds(pl.multiple_of(number * shard, shard), shard)

    def columns_of(peer_seq, head):
        return pl.ds(pl.multiple_of(peer_seq * (heads * HEAD) + head * HEAD, HEAD), HEAD)

    def greet(semaphore, along_seq, along_bal):
        peer = at(along_seq, along_bal)
        pl.semaphore_signal(semaphore, inc=1, device_id=device(peer), device_id_type=MESH)

    everything, early, late = (0, views), (0, views // 2), (views // 2, views - views // 2)
    inbound = []
    for head, source, landing, part in (
        (0, keys, k0, everything),
        (0, values, v0, everything),
        (0, queries, q0, everything),
        (1, keys, k1, everything),
        (1, values, v1, everything),
        (1, queries, q1, early),
        (1, queries, q1, late),
    ):
        inbound.append((head, len(inbound), source, landing, pl.ds(*part)))

    def send(piece, along_seq, along_bal):
        head, number, source, landing, part = piece
        peer = at(along_seq, along_bal)
        pltpu.make_async_remote_copy(
            src_ref=source.at[peer[1], part, :, columns_of(peer[0], head)],
            dst_ref=landing.at[part, rows_of(me), :],
            send_sem=send_in.at[number],
            recv_sem=recv_in.at[number],
            device_id=device(peer),
            device_id_type=MESH,
        ).start()

    def keep(piece):
        head, number, source, landing, part = piece
        pltpu.make_async_copy(
            source.at[bal, part, :, columns_of(seq, head)], landing.at[part, rows_of(me), :], recv_in.at[number]
        ).start()

    lists = pltpu.make_async_copy(lists_in, view_lists, lists_sem)
    lists.start()

    barrier = pltpu.get_barrier_semaphore()
    loop(1, seq_count, lambda dz: greet(barrier, dz, 0))
    loop(1, bal_count, lambda dx: greet(barrier, 0, dx))
    pl.semaphore_wait(barrier, seq_count + bal_count - 2)
    loop(1, bal_count, lambda dx: greet(columns_in, 0, dx))
    loop(1, seq_count, lambda dz: send(inbound[0], dz, 0))
    loop(1, bal_count, lambda dx: send(inbound[0], 0, dx))
    keep(inbound[0])
    pl.semaphore_wait(columns_in, bal_count - 1)

    loop(1, seq_count, lambda dz: loop(1, bal_count, lambda dx: send(inbound[0], dz, dx)))
    for piece in inbound[1:]:
        loop(1, peers, lambda step: send(piece, lax.div(step, bal_count), lax.rem(step, bal_count)))
        keep(piece)

    def arrive(piece):
        head, number, source, landing, part = piece
        whole = landing.at[part]
        pltpu.make_async_copy(whole, whole, recv_in.at[number]).wait()

    def give_back(head, result, view):
        def give(step):
            other = jnp.where(step - 1 >= me, step, step - 1)
            peer = lax.div(other, bal_count), lax.rem(other, bal_count)
            pltpu.make_async_remote_copy(
                src_ref=result.at[view, rows_of(peer[0] * bal_count + peer[1]), :],
                dst_ref=out.at[bal, view, :, columns_of(seq, head)],
                send_sem=send_out,
                recv_sem=recv_out,
                device_id=device(peer),
                device_id_type=MESH,
            ).start()

        loop(1, peers, give)
        pltpu.make_async_copy(
            result.at[view, rows_of(me), :], out.at[bal, view, :, columns_of(seq, head)], recv_out
        ).start()

    for piece in inbound[:3]:
        arrive(piece)

    lists.wait()

    def first_head(view):
        attend(view_lists, bal, view, q0, k0, v0, r0)
        give_back(0, r0, view)

    loop(0, views, first_head)
    for piece in inbound[3:6]:
        arrive(piece)

    def second_head(view):
        attend(view_lists, bal, view, q1, k1, v1, r1)
        give_back(1, r1, view)

    loop(0, early[1], second_head)
    arrive(inbound[6])
    loop(early[1], views, second_head)

    pltpu.make_async_copy(out, out, recv_out).wait()
    for head, number, source, landing, part in inbound:
        sent = landing.at[part, pl.ds(0, window_rows - shard), :]
        pltpu.make_async_copy(sent, sent, send_in.at[number]).wait()
    for result in (r0, r1):
        sent = result.at[:, pl.ds(0, window_rows - shard), :]
        pltpu.make_async_copy(sent, sent, send_out).wait()


def local(seq_count, bal_count, queries, key_tokens, value_tokens, view_lists):
    windows, views, shard, width = queries.shape
    window_rows = seq_count * bal_count * shard
    head_buffer = pltpu.VMEM((views, window_rows, HEAD), jnp.bfloat16)
    return pl.pallas_call(
        functools.partial(kernel, seq_count, bal_count),
        out_shape=pltpu.VMEM(queries.shape, jnp.bfloat16),
        in_specs=[pl.BlockSpec(memory_space=pl.ANY)] * 4,
        scratch_shapes=[head_buffer] * 8
        + [
            pltpu.SemaphoreType.DMA((7,)),
            pltpu.SemaphoreType.DMA((7,)),
            pltpu.SemaphoreType.DMA,
            pltpu.SemaphoreType.DMA,
            pltpu.SemaphoreType.REGULAR,
            pltpu.SMEM((windows, view_lists.shape[2], views), jnp.int32),
            pltpu.SemaphoreType.DMA,
        ],
        compiler_params=pltpu.CompilerParams(
            collective_id=0, has_side_effects=True, vmem_limit_bytes=62 * 2**20
        ),
    )(jnp.swapaxes(view_lists, 1, 2), queries, key_tokens, value_tokens)


def solution(mesh):
    spec = P("rep", None, ("seq", "bal"), None)
    return jax.shard_map(
        functools.partial(local, mesh.shape["seq"], mesh.shape["bal"]),
        mesh=mesh,
        in_specs=(spec, spec, spec, P("rep", None, None)),
        out_specs=spec,
        check_vma=False,
    )
```

```python
import functools
import math

import jax
import jax.numpy as jnp
from jax import lax
from jax.experimental import pallas as pl
from jax.experimental.pallas import tpu as pltpu
from jax.sharding import PartitionSpec as P

HEAD = 128
QUERY_BLOCK = 256
MESH = pl.DeviceIdType.MESH
ROWS_BY_ROWS = (((1,), (1,)), ((), ()))
EXP2_SCALE = math.log2(math.e) / math.sqrt(HEAD)


def attend(view_lists, window, view, query_buf, key_buf, value_buf, result_buf):
    slots = view_lists.shape[1]
    rows = query_buf.shape[1]
    entries = [view_lists[window, slot, view] for slot in range(slots)]
    named = [jnp.where(entry >= 0, 1.0, 0.0).astype(jnp.float32) for entry in entries]
    key_views = [jnp.where(entry >= 0, entry, view) for entry in entries]

    def block(index, carry):
        span = pl.ds(pl.multiple_of(index * QUERY_BLOCK, QUERY_BLOCK), QUERY_BLOCK)
        query_rows = query_buf[view, span, :]
        scores = [
            lax.dot_general(query_rows, key_buf[u], ROWS_BY_ROWS, preferred_element_type=jnp.float32)
            for u in key_views
        ]
        top = functools.reduce(jnp.maximum, scores)
        top = jnp.max(top, axis=1, keepdims=True) * EXP2_SCALE
        total = jnp.zeros((QUERY_BLOCK, 1), jnp.float32)
        mixed = jnp.zeros((QUERY_BLOCK, HEAD), jnp.float32)
        for slot, u in enumerate(key_views):
            exponent = jnp.exp2(scores[slot] * EXP2_SCALE - top)
            total += jnp.sum(exponent, axis=1, keepdims=True) * named[slot]
            values = value_buf[u] * named[slot].astype(jnp.bfloat16)
            mixed += jnp.dot(exponent.astype(jnp.bfloat16), values, preferred_element_type=jnp.float32)
        result_buf[view, span, :] = (mixed / total).astype(jnp.bfloat16)
        return carry

    lax.fori_loop(0, rows // QUERY_BLOCK, block, 0)


def kernel(
    seq_count, bal_count,
    lists_in, queries_in, keys_in, values_in,
    out,
    q0, q1, k0, k1, v0, v1, r0, r1,
    send_in, recv_in, send_out, recv_out, columns_in,
    view_lists, lists_sem, queries, keys, values, staged,
):
    stages = [
        pltpu.make_async_copy(given, copy, staged.at[number])
        for number, (given, copy) in enumerate(((keys_in, keys), (values_in, values), (queries_in, queries)))
    ]
    for stage in stages:
        stage.start()

    seq, bal = lax.axis_index("seq"), lax.axis_index("bal")
    peers = seq_count * bal_count
    me = seq * bal_count + bal
    shard = queries.shape[2]
    views = queries.shape[1]
    heads = 2
    window_rows = peers * shard

    def loop(first, last, body):
        def run(index, carry):
            body(index)
            return carry

        lax.fori_loop(first, last, run, 0)

    def at(along_seq, along_bal):
        return lax.rem(seq + along_seq, seq_count), lax.rem(bal + along_bal, bal_count)

    def device(peer):
        return {"seq": peer[0], "bal": peer[1]}

    def rows_of(number):
        return pl.ds(pl.multiple_of(number * shard, shard), shard)

    def columns_of(peer_seq, head):
        return pl.ds(pl.multiple_of(peer_seq * (heads * HEAD) + head * HEAD, HEAD), HEAD)

    def greet(semaphore, along_seq, along_bal):
        peer = at(along_seq, along_bal)
        pl.semaphore_signal(semaphore, inc=1, device_id=device(peer), device_id_type=MESH)

    everything, early, late = (0, views), (0, views // 2), (views // 2, views - views // 2)
    inbound = []
    for head, source, landing, part in (
        (0, keys, k0, everything),
        (0, values, v0, everything),
        (0, queries, q0, everything),
        (1, keys, k1, everything),
        (1, values, v1, everything),
        (1, queries, q1, early),
        (1, queries, q1, late),
    ):
        inbound.append((head, len(inbound), source, landing, pl.ds(*part)))

    def send(piece, along_seq, along_bal):
        head, number, source, landing, part = piece
        peer = at(along_seq, along_bal)
        pltpu.make_async_remote_copy(
            src_ref=source.at[peer[1], part, :, columns_of(peer[0], head)],
            dst_ref=landing.at[part, rows_of(me), :],
            send_sem=send_in.at[number],
            recv_sem=recv_in.at[number],
            device_id=device(peer),
            device_id_type=MESH,
        ).start()

    def keep(piece):
        head, number, source, landing, part = piece
        pltpu.make_async_copy(
            source.at[bal, part, :, columns_of(seq, head)], landing.at[part, rows_of(me), :], recv_in.at[number]
        ).start()

    lists = pltpu.make_async_copy(lists_in, view_lists, lists_sem)
    lists.start()

    barrier = pltpu.get_barrier_semaphore()
    loop(1, seq_count, lambda dz: greet(barrier, dz, 0))
    loop(1, bal_count, lambda dx: greet(barrier, 0, dx))
    pl.semaphore_wait(barrier, seq_count + bal_count - 2)
    loop(1, bal_count, lambda dx: greet(columns_in, 0, dx))
    stages[0].wait()
    loop(1, seq_count, lambda dz: send(inbound[0], dz, 0))
    loop(1, bal_count, lambda dx: send(inbound[0], 0, dx))
    keep(inbound[0])
    pl.semaphore_wait(columns_in, bal_count - 1)

    loop(1, seq_count, lambda dz: loop(1, bal_count, lambda dx: send(inbound[0], dz, dx)))
    for piece in inbound[1:]:
        if piece[1] < len(stages):
            stages[piece[1]].wait()
        loop(1, peers, lambda step: send(piece, lax.div(step, bal_count), lax.rem(step, bal_count)))
        keep(piece)

    def arrive(piece):
        head, number, source, landing, part = piece
        whole = landing.at[part]
        pltpu.make_async_copy(whole, whole, recv_in.at[number]).wait()

    def give_back(head, result, view):
        def give(step):
            half = peers // 2
            low = jnp.where(step - 1 >= me, step, step - 1)
            high = half + lax.rem(me + step - half, half)
            other = jnp.where(step < half + jnp.where(me >= half, 1, 0), low, high)
            peer = lax.div(other, bal_count), lax.rem(other, bal_count)
            pltpu.make_async_remote_copy(
                src_ref=result.at[view, rows_of(peer[0] * bal_count + peer[1]), :],
                dst_ref=out.at[bal, view, :, columns_of(seq, head)],
                send_sem=send_out,
                recv_sem=recv_out,
                device_id=device(peer),
                device_id_type=MESH,
            ).start()

        loop(1, peers, give)
        pltpu.make_async_copy(
            result.at[view, rows_of(me), :], out.at[bal, view, :, columns_of(seq, head)], recv_out
        ).start()

    for piece in inbound[:3]:
        arrive(piece)

    lists.wait()

    def first_head(view):
        attend(view_lists, bal, view, q0, k0, v0, r0)
        give_back(0, r0, view)

    loop(0, views, first_head)
    for piece in inbound[3:6]:
        arrive(piece)

    def second_head(view):
        attend(view_lists, bal, view, q1, k1, v1, r1)
        give_back(1, r1, view)

    loop(0, early[1], second_head)
    arrive(inbound[6])
    loop(early[1], views, second_head)

    pltpu.make_async_copy(out, out, recv_out).wait()
    for head, number, source, landing, part in inbound:
        sent = landing.at[part, pl.ds(0, window_rows - shard), :]
        pltpu.make_async_copy(sent, sent, send_in.at[number]).wait()
    for result in (r0, r1):
        sent = result.at[:, pl.ds(0, window_rows - shard), :]
        pltpu.make_async_copy(sent, sent, send_out).wait()


def local(seq_count, bal_count, queries, key_tokens, value_tokens, view_lists):
    windows, views, shard, width = queries.shape
    window_rows = seq_count * bal_count * shard
    head_buffer = pltpu.VMEM((views, window_rows, HEAD), jnp.bfloat16)
    return pl.pallas_call(
        functools.partial(kernel, seq_count, bal_count),
        out_shape=pltpu.VMEM(queries.shape, jnp.bfloat16),
        in_specs=[pl.BlockSpec(memory_space=pl.ANY)] * 4,
        scratch_shapes=[head_buffer] * 8
        + [
            pltpu.SemaphoreType.DMA((7,)),
            pltpu.SemaphoreType.DMA((7,)),
            pltpu.SemaphoreType.DMA,
            pltpu.SemaphoreType.DMA,
            pltpu.SemaphoreType.REGULAR,
            pltpu.SMEM((windows, view_lists.shape[2], views), jnp.int32),
            pltpu.SemaphoreType.DMA,
        ]
        + [pltpu.VMEM(queries.shape, jnp.bfloat16)] * 3
        + [
            pltpu.SemaphoreType.DMA((3,)),
        ],
        compiler_params=pltpu.CompilerParams(
            collective_id=0, has_side_effects=True, vmem_limit_bytes=62 * 2**20
        ),
    )(jnp.swapaxes(view_lists, 1, 2), queries, key_tokens, value_tokens)


def solution(mesh):
    spec = P("rep", None, ("seq", "bal"), None)
    return jax.shard_map(
        functools.partial(local, mesh.shape["seq"], mesh.shape["bal"]),
        mesh=mesh,
        in_specs=(spec, spec, spec, P("rep", None, None)),
        out_specs=spec,
        check_vma=False,
    )
```

```python
import functools
import math

import jax
import jax.numpy as jnp
from jax import lax
from jax.experimental import pallas as pl
from jax.experimental.pallas import tpu as pltpu
from jax.sharding import PartitionSpec as P

HEAD = 128
QUERY_BLOCK = 256
MESH = pl.DeviceIdType.MESH
ROWS_BY_ROWS = (((1,), (1,)), ((), ()))
EXP2_SCALE = math.log2(math.e) / math.sqrt(HEAD)


def attend(view_lists, window, view, query_buf, key_buf, value_buf, result_buf):
    slots = view_lists.shape[1]
    rows = query_buf.shape[1]
    entries = [view_lists[window, slot, view] for slot in range(slots)]
    named = [jnp.where(entry >= 0, 1.0, 0.0).astype(jnp.float32) for entry in entries]
    key_views = [jnp.where(entry >= 0, entry, view) for entry in entries]

    def block(index, carry):
        span = pl.ds(pl.multiple_of(index * QUERY_BLOCK, QUERY_BLOCK), QUERY_BLOCK)
        query_rows = query_buf[view, span, :]
        scores = [
            lax.dot_general(query_rows, key_buf[u], ROWS_BY_ROWS, preferred_element_type=jnp.float32)
            for u in key_views
        ]
        top = functools.reduce(jnp.maximum, scores)
        top = jnp.max(top, axis=1, keepdims=True) * EXP2_SCALE
        total = jnp.zeros((QUERY_BLOCK, 1), jnp.float32)
        mixed = jnp.zeros((QUERY_BLOCK, HEAD), jnp.float32)
        for slot, u in enumerate(key_views):
            exponent = jnp.exp2(scores[slot] * EXP2_SCALE - top)
            total += jnp.sum(exponent, axis=1, keepdims=True) * named[slot]
            values = value_buf[u] * named[slot].astype(jnp.bfloat16)
            mixed += jnp.dot(exponent.astype(jnp.bfloat16), values, preferred_element_type=jnp.float32)
        result_buf[view, span, :] = (mixed / total).astype(jnp.bfloat16)
        return carry

    lax.fori_loop(0, rows // QUERY_BLOCK, block, 0)


def kernel(
    seq_count, bal_count,
    lists_in, queries_in, keys_in, values_in,
    out,
    q0, q1, k0, k1, v0, v1, r0, r1,
    send_in, recv_in, send_out, recv_out, columns_in, near_in, far_in,
    view_lists, lists_sem, queries, keys, values, staged,
):
    stages = [
        pltpu.make_async_copy(given, copy, staged.at[number])
        for number, (given, copy) in enumerate(((keys_in, keys), (values_in, values), (queries_in, queries)))
    ]
    for stage in stages:
        stage.start()

    seq, bal = lax.axis_index("seq"), lax.axis_index("bal")
    peers = seq_count * bal_count
    me = seq * bal_count + bal
    shard = queries.shape[2]
    views = queries.shape[1]
    heads = 2
    window_rows = peers * shard

    def loop(first, last, body):
        def run(index, carry):
            body(index)
            return carry

        lax.fori_loop(first, last, run, 0)

    def at(along_seq, along_bal):
        return lax.rem(seq + along_seq, seq_count), lax.rem(bal + along_bal, bal_count)

    def device(peer):
        return {"seq": peer[0], "bal": peer[1]}

    def rows_of(number):
        return pl.ds(pl.multiple_of(number * shard, shard), shard)

    def columns_of(peer_seq, head):
        return pl.ds(pl.multiple_of(peer_seq * (heads * HEAD) + head * HEAD, HEAD), HEAD)

    def greet(semaphore, along_seq, along_bal):
        peer = at(along_seq, along_bal)
        pl.semaphore_signal(semaphore, inc=1, device_id=device(peer), device_id_type=MESH)

    everything, early, late = (0, views), (0, views // 2), (views // 2, views - views // 2)
    inbound = []
    for head, source, landing, part in (
        (0, keys, k0, everything),
        (0, values, v0, everything),
        (0, queries, q0, everything),
        (1, keys, k1, everything),
        (1, values, v1, everything),
        (1, queries, q1, early),
        (1, queries, q1, late),
    ):
        inbound.append((head, len(inbound), source, landing, pl.ds(*part)))

    def send(piece, along_seq, along_bal):
        head, number, source, landing, part = piece
        peer = at(along_seq, along_bal)
        pltpu.make_async_remote_copy(
            src_ref=source.at[peer[1], part, :, columns_of(peer[0], head)],
            dst_ref=landing.at[part, rows_of(me), :],
            send_sem=send_in.at[number],
            recv_sem=recv_in.at[number],
            device_id=device(peer),
            device_id_type=MESH,
        ).start()

    def keep(piece):
        head, number, source, landing, part = piece
        pltpu.make_async_copy(
            source.at[bal, part, :, columns_of(seq, head)], landing.at[part, rows_of(me), :], recv_in.at[number]
        ).start()

    lists = pltpu.make_async_copy(lists_in, view_lists, lists_sem)
    lists.start()

    first = inbound[0]
    far = seq_count // 2

    def both(distance, body):
        body(distance)
        body(seq_count - distance)

    def row(dz):
        loop(1, bal_count, lambda dx: send(first, dz, dx))

    barrier = pltpu.get_barrier_semaphore()
    both(1, lambda dz: greet(barrier, dz, 0))
    loop(1, bal_count, lambda dx: greet(barrier, 0, dx))
    pl.semaphore_wait(barrier, bal_count + 1)
    both(1, lambda dz: greet(near_in, dz, 0))
    stages[0].wait()
    both(1, lambda dz: send(first, dz, 0))
    row(0)
    keep(first)
    pl.semaphore_wait(near_in, 2)
    both(2, lambda dz: greet(far_in, dz, 0))
    both(2, lambda dz: send(first, dz, 0))
    both(1, row)
    pl.semaphore_wait(far_in, 2)
    loop(1, bal_count, lambda dx: greet(columns_in, 0, dx))
    both(3, lambda dz: send(first, dz, 0))
    send(first, far, 0)
    both(2, row)
    both(3, row)
    pl.semaphore_wait(columns_in, bal_count - 1)
    row(far)

    for piece in inbound[1:]:
        if piece[1] < len(stages):
            stages[piece[1]].wait()
        loop(1, peers, lambda step: send(piece, lax.div(step, bal_count), lax.rem(step, bal_count)))
        keep(piece)

    def arrive(piece):
        head, number, source, landing, part = piece
        whole = landing.at[part]
        pltpu.make_async_copy(whole, whole, recv_in.at[number]).wait()

    def give_back(head, result, view):
        def give(step):
            half = peers // 2
            low = jnp.where(step - 1 >= me, step, step - 1)
            high = half + lax.rem(me + step - half, half)
            other = jnp.where(step < half + jnp.where(me >= half, 1, 0), low, high)
            peer = lax.div(other, bal_count), lax.rem(other, bal_count)
            pltpu.make_async_remote_copy(
                src_ref=result.at[view, rows_of(peer[0] * bal_count + peer[1]), :],
                dst_ref=out.at[bal, view, :, columns_of(seq, head)],
                send_sem=send_out,
                recv_sem=recv_out,
                device_id=device(peer),
                device_id_type=MESH,
            ).start()

        loop(1, peers, give)
        pltpu.make_async_copy(
            result.at[view, rows_of(me), :], out.at[bal, view, :, columns_of(seq, head)], recv_out
        ).start()

    for piece in inbound[:3]:
        arrive(piece)

    lists.wait()

    def first_head(view):
        attend(view_lists, bal, view, q0, k0, v0, r0)
        give_back(0, r0, view)

    loop(0, views, first_head)
    for piece in inbound[3:6]:
        arrive(piece)

    def second_head(view):
        attend(view_lists, bal, view, q1, k1, v1, r1)
        give_back(1, r1, view)

    loop(0, early[1], second_head)
    arrive(inbound[6])
    loop(early[1], views, second_head)

    pltpu.make_async_copy(out, out, recv_out).wait()
    for head, number, source, landing, part in inbound:
        sent = landing.at[part, pl.ds(0, window_rows - shard), :]
        pltpu.make_async_copy(sent, sent, send_in.at[number]).wait()
    for result in (r0, r1):
        sent = result.at[:, pl.ds(0, window_rows - shard), :]
        pltpu.make_async_copy(sent, sent, send_out).wait()


def local(seq_count, bal_count, queries, key_tokens, value_tokens, view_lists):
    windows, views, shard, width = queries.shape
    window_rows = seq_count * bal_count * shard
    head_buffer = pltpu.VMEM((views, window_rows, HEAD), jnp.bfloat16)
    return pl.pallas_call(
        functools.partial(kernel, seq_count, bal_count),
        out_shape=pltpu.VMEM(queries.shape, jnp.bfloat16),
        in_specs=[pl.BlockSpec(memory_space=pl.ANY)] * 4,
        scratch_shapes=[head_buffer] * 8
        + [
            pltpu.SemaphoreType.DMA((7,)),
            pltpu.SemaphoreType.DMA((7,)),
            pltpu.SemaphoreType.DMA,
            pltpu.SemaphoreType.DMA,
            pltpu.SemaphoreType.REGULAR,
            pltpu.SemaphoreType.REGULAR,
            pltpu.SemaphoreType.REGULAR,
            pltpu.SMEM((windows, view_lists.shape[2], views), jnp.int32),
            pltpu.SemaphoreType.DMA,
        ]
        + [pltpu.VMEM(queries.shape, jnp.bfloat16)] * 3
        + [
            pltpu.SemaphoreType.DMA((3,)),
        ],
        compiler_params=pltpu.CompilerParams(
            collective_id=0, has_side_effects=True, vmem_limit_bytes=62 * 2**20
        ),
    )(jnp.swapaxes(view_lists, 1, 2), queries, key_tokens, value_tokens)


def solution(mesh):
    spec = P("rep", None, ("seq", "bal"), None)
    return jax.shard_map(
        functools.partial(local, mesh.shape["seq"], mesh.shape["bal"]),
        mesh=mesh,
        in_specs=(spec, spec, spec, P("rep", None, None)),
        out_specs=spec,
        check_vma=False,
    )
```
